256 devices in a mesh: block: 64 (over z, y_lo, x), tok: 4 (over y_hi, core).
Axes of the slice: x: 4, y: 4 (y_hi: 2, y_lo: 2; y = y_hi * 2 + y_lo), z: 8, core: 2. Of those that a mesh axis runs over, the one named last changes fastest.
Arguments:
- fast_in: float32 [64, 4, 3, 512, 512], P('block', 'tok'), may hold values from -0.25 to 0.25
- queries: bfloat16 [3, 64, 512, 2048], P(None, 'block', 'tok'), may hold values from -6 to 6
- keys: bfloat16 [3, 64, 512, 2048], P(None, 'block', 'tok'), may hold values from -6 to 6
- values: bfloat16 [3, 64, 512, 2048], P(None, 'block', 'tok'), may hold values from -6 to 6
- rates: bfloat16 [3, 64, 512, 4], P(None, 'block', 'tok'), may hold values from 0.0009765625 to 0.0078125
Outputs:
- outputs: bfloat16 [3, 64, 512, 2048], P(None, 'block', 'tok')
- fast_out: float32 [64, 4, 3, 512, 512], P('block', 'tok')
The draws below stay inside these ranges and needn't reach their ends.
All inputs are finite; a program needn't handle non-finite values.
Results may differ from the reference program's by a relative error of at most 0.002.
Values may be sent and summed in bfloat16 or wider, within the bound.
No kernel may reach another device: no remote copies, remote signals or barrier semaphores. Data moves between devices by JAX's collectives and lax.ppermute only.
A program may use at most 128 MiB of HBM per device.

```python
import math
import jax
import jax.numpy as jnp
from jax import lax

HEADS = 4
DH = 512
STEPS = 3
BLOCK = 512
OWNERS = 64
WIDTH = 2048


def level_of(rng, dims, split, low, high):
    gain, own = 1.0, jax.random.fold_in(rng, 6)
    for axis_at, blocks in split:
        steps = jnp.exp(jax.random.uniform(jax.random.fold_in(own, axis_at), (blocks,), jnp.float32, low / len(split), high / len(split)))
        gain = gain * jnp.repeat(steps, dims[axis_at] // blocks).reshape([-1 if axis == axis_at else 1 for axis in range(len(dims))])
    return gain


def scatter_about(own_key, dims, scale, reach, cuts=(), held_as=jnp.bfloat16):
    values = scale * jax.random.normal(own_key, dims, jnp.float32)
    if cuts:
        values = values * level_of(own_key, dims, cuts, -0.22, 0.18)
    return jnp.clip(values, -reach, reach).astype(held_as)


def setup_inputs(seed: int = 0) -> dict:
    arg_keys = jax.random.split(jax.random.key(seed), 6)
    fast_in = scatter_about(arg_keys[0], (OWNERS, HEADS, 3, DH, DH), DH ** -0.5, 0.25, ((0, 64), (1, 4)), jnp.float32)
    queries = scatter_about(arg_keys[1], (STEPS, OWNERS, BLOCK, WIDTH), 1.0, 6.0, ((1, 64), (2, 4)))
    keys = scatter_about(arg_keys[2], (STEPS, OWNERS, BLOCK, WIDTH), 1.0, 6.0, ((1, 64), (2, 4)))
    values = scatter_about(arg_keys[3], (STEPS, OWNERS, BLOCK, WIDTH), 1.0, 6.0, ((1, 64), (2, 4)))
    rates = jnp.clip(jnp.exp(math.log(0.0078125) - 2.0794415 * jax.random.uniform(arg_keys[4], (STEPS, OWNERS, BLOCK, HEADS), jnp.float32) ** level_of(arg_keys[4], (STEPS, OWNERS, BLOCK, HEADS), ((1, 64), (2, 4)), -0.2, 0.2)), 0.0009765625, 0.0078125).astype(jnp.bfloat16)
    return dict(fast_in=fast_in, queries=queries, keys=keys, values=values, rates=rates)


precise = lax.Precision.HIGHEST
epsilon = 1e-06

def renormed(initial, stepped):
    rescale = jnp.sqrt((lax.optimization_barrier(jnp.mean(initial * initial, axis=-1)) + epsilon) / (lax.optimization_barrier(jnp.mean(stepped * stepped, axis=-1)) + epsilon))
    return stepped * rescale[..., None]

def fast_update(weights, key_full, value_full, rate_full):
    hidden = jnp.einsum('thd,hdf->thf', key_full, weights[:, 0], precision=precise)
    gated = jnp.einsum('thd,hdf->thf', key_full, weights[:, 1], precision=precise)
    gate_sig = jax.nn.sigmoid(hidden)
    active = hidden * gate_sig
    target = -rate_full[:, :, None] * value_full
    grad_down = jnp.einsum('thf,the->hfe', active * gated, target, precision=precise)
    back_grad = jnp.einsum('the,hfe->thf', target, weights[:, 2], precision=precise)
    grad_first = jnp.einsum('thd,thf->hdf', key_full, back_grad * gated * gate_sig * (1.0 + hidden * (1.0 - gate_sig)), precision=precise)
    grad_gate = jnp.einsum('thd,thf->hdf', key_full, back_grad * active, precision=precise)
    new_down = renormed(weights[:, 2], weights[:, 2] - grad_down)
    new_inner = renormed(weights[:, :2], weights[:, :2] - jnp.stack([grad_first, grad_gate], axis=1))
    return jnp.concatenate([new_inner, new_down[:, None]], axis=1)

def apply_fast(updated, query_full):
    hidden = jnp.einsum('thd,hdf->thf', query_full, updated[:, 0], precision=precise)
    gated = jnp.einsum('thd,hdf->thf', query_full, updated[:, 1], precision=precise)
    return jnp.einsum('thf,hfe->the', jax.nn.silu(hidden) * gated, updated[:, 2], precision=precise)

def reference(fast_in, queries, keys, values, rates):
    head_count = fast_in.shape[1]
    head_width = fast_in.shape[3]
    block_len = queries.shape[2]
    current = fast_in
    results = []
    for round_index in range(STEPS):
        if round_index > 0:
            current = jnp.roll(current, 1, axis=0)

        def one_owner(packed):
            weights, query_now, key_now, value_now, rate_now = packed
            query_full = query_now.astype(jnp.float32).reshape(block_len, head_count, head_width)
            key_full = key_now.astype(jnp.float32).reshape(block_len, head_count, head_width)
            value_full = value_now.astype(jnp.float32).reshape(block_len, head_count, head_width)
            rate_full = rate_now.astype(jnp.float32)
            updated = fast_update(weights, key_full, value_full, rate_full)
            result = apply_fast(updated, query_full).reshape(block_len, head_count * head_width).astype(jnp.bfloat16)
            return (updated, result)
        current, result = lax.map(one_owner, (current, queries[round_index], keys[round_index], values[round_index], rates[round_index]))
        results.append(result)
    return (jnp.stack(results, axis=0), current)
```

```python
import functools

import jax
import jax.numpy as jnp
from jax import lax
from jax.experimental import pallas as pl
from jax.experimental.pallas import tpu as pltpu
from jax.sharding import PartitionSpec as P

F32 = jnp.float32
BF16 = jnp.bfloat16
WIRE = jnp.float16
WIRE_SCALE = 8192.0
EPS = 1e-06
NN = ((1,), (0,))
NT = ((1,), (1,))
TN = ((0,), (0,))
PIECES = 4
BOTH = ("block", "tok")


def dot(a, b, dims):
    return lax.dot_general(a, b, (dims, ((), ())), preferred_element_type=F32)


def halves(x):
    high = x.astype(BF16)
    return high, (x - high.astype(F32)).astype(BF16)


def dot_exact_left(a, b, dims):
    high, low = halves(b)
    return dot(a, high, dims) + dot(a, low, dims)


def renormed(initial, stepped):
    before = jnp.mean(initial * initial, axis=-1, keepdims=True) + EPS
    after = jnp.mean(stepped * stepped, axis=-1, keepdims=True) + EPS
    return stepped * jnp.sqrt(before / after)


def diagonal(n):
    return lax.broadcasted_iota(jnp.int32, (n, n), 0) == lax.broadcasted_iota(jnp.int32, (n, n), 1)


def as_column(row):
    n = row.shape[1]
    return jnp.sum(jnp.where(diagonal(n), jnp.broadcast_to(row, (n, n)), 0.0), axis=1, keepdims=True)


def as_row(column):
    n = column.shape[0]
    return jnp.sum(jnp.where(diagonal(n), jnp.broadcast_to(column, (n, n)), 0.0), axis=0, keepdims=True)


def pack_kernel(count, steps, tok_ref, *refs):
    rates_ref = refs[count * PIECES] if steps else None
    outs = refs[-PIECES:]
    for p in range(PIECES):
        for i in range(count):
            outs[p][i * 128 : (i + 1) * 128] = refs[i * PIECES + p][0, 0]
        if steps:
            rows = []
            for s in range(steps):
                rate = rates_ref[s, 0].astype(F32)
                head = lax.broadcasted_iota(jnp.int32, rate.shape, 1)
                mine = jnp.sum(jnp.where(head == (tok_ref[0] ^ p), rate, 0.0), axis=1, keepdims=True)
                rows.append(as_row(mine))
            slab = jnp.concatenate(rows + [jnp.zeros((16 - steps, 128), F32)], axis=0)
            slab = jnp.concatenate([slab, jnp.zeros((16, 384), F32)], axis=1)
            outs[p][count * 128 :] = slab.astype(BF16)


def pack(tok, items, rates=None):
    count = len(items)
    specs, operands = [], []
    for array, step in items:
        for p in range(PIECES):
            specs.append(
                pl.BlockSpec((1, 1, 128, 512), lambda i, t, step=step, p=p: (step, 0, 0, t[0] ^ p))
            )
            operands.append(array)
    steps = 0
    rows = count * 128
    if rates is not None:
        steps = rates.shape[0]
        rows += 16
        specs.append(pl.BlockSpec(rates.shape, lambda i, t: (0, 0, 0, 0)))
        operands.append(rates)
    return pl.pallas_call(
        functools.partial(pack_kernel, count, steps),
        grid_spec=pltpu.PrefetchScalarGridSpec(
            num_scalar_prefetch=1,
            grid=(1,),
            in_specs=specs,
            out_specs=[pl.BlockSpec((rows, 512), lambda i, t: (0, 0))] * PIECES,
        ),
        out_shape=[jax.ShapeDtypeStruct((rows, 512), BF16)] * PIECES,
        name="pack",
    )(tok, *operands)


def update_kernel(step, offset, w_ref, *refs):
    data, rates, u_ref = refs[:PIECES], refs[PIECES : 2 * PIECES], refs[2 * PIECES]
    first, gate, down = w_ref[0], w_ref[1], w_ref[2]
    k = jnp.concatenate([d[offset : offset + 128] for d in data], axis=0)
    v = jnp.concatenate([d[offset + 128 : offset + 256] for d in data], axis=0)
    minus_eta = jnp.concatenate(
        [-as_column(r[256 + step : 257 + step, 0:128].astype(F32)) for r in rates], axis=0
    )
    hidden = dot_exact_left(k, first, NN)
    gated = dot_exact_left(k, gate, NN)
    sig = jax.nn.sigmoid(hidden)
    active = hidden * sig
    back = minus_eta * dot_exact_left(v, down, NT)
    high, low = halves(active * gated * minus_eta)
    u_ref[2] = renormed(down, down - (dot(high, v, TN) + dot(low, v, TN)))
    slope = back * gated * sig * (1.0 + hidden * (1.0 - sig))
    u_ref[0] = renormed(first, first - dot_exact_left(k, slope, TN))
    u_ref[1] = renormed(gate, gate - dot_exact_left(k, back * active, TN))


def update(weights, data, rates, step, offset):
    return pl.pallas_call(
        functools.partial(update_kernel, step, offset),
        out_shape=jax.ShapeDtypeStruct(weights.shape, F32),
        compiler_params=pltpu.CompilerParams(vmem_limit_bytes=40 << 20),
        name="update",
    )(weights, *data, *rates)


def apply_kernel(offset, u_ref, *refs):
    data, outs = refs[:PIECES], refs[PIECES:]
    q = jnp.concatenate([d[offset : offset + 128] for d in data], axis=0)
    hidden = dot_exact_left(q, u_ref[0], NN)
    gated = dot_exact_left(q, u_ref[1], NN)
    ah, al = halves(hidden * jax.nn.sigmoid(hidden) * gated)
    uh, ul = halves(u_ref[2])
    result = dot(ah, uh, NN) + (dot(ah, ul, NN) + dot(al, uh, NN))
    for p in range(PIECES):
        outs[p][...] = result[p * 128 : (p + 1) * 128].astype(BF16)


def apply_fast(updated, data, offset):
    return pl.pallas_call(
        functools.partial(apply_kernel, offset),
        out_shape=[jax.ShapeDtypeStruct((128, 512), BF16)] * PIECES,
        compiler_params=pltpu.CompilerParams(vmem_limit_bytes=40 << 20),
        name="apply",
    )(updated, *data)


def place_kernel(aliased, tok_ref, *refs):
    pieces, out_ref = refs[aliased : aliased + PIECES], refs[-1]
    for p in range(PIECES):

        @pl.when(pl.program_id(0) == p)
        def _():
            out_ref[0, 0] = pieces[p][...]


def place(tok, pieces, step, steps, so_far):
    aliased = 0 if so_far is None else 1
    specs = [pl.BlockSpec(memory_space=pl.ANY)] * aliased
    specs += [pl.BlockSpec((128, 512), lambda i, t: (0, 0))] * PIECES
    operands = ([] if so_far is None else [so_far]) + list(pieces)
    return pl.pallas_call(
        functools.partial(place_kernel, aliased),
        grid_spec=pltpu.PrefetchScalarGridSpec(
            num_scalar_prefetch=1,
            grid=(PIECES,),
            in_specs=specs,
            out_specs=pl.BlockSpec((1, 1, 128, 512), lambda i, t: (step, 0, 0, t[0] ^ i)),
        ),
        out_shape=jax.ShapeDtypeStruct((steps, 1, 128, 2048), BF16),
        input_output_aliases={1: 0} if aliased else {},
        name="place",
    )(tok, *operands)


def exchange(pieces):
    out = [pieces[0]]
    for p in range(1, PIECES):
        out.append(lax.ppermute(pieces[p], "tok", [(i, i ^ p) for i in range(PIECES)]))
    return out


def handed_on(updated):
    count = lax.axis_size("block")
    sent = (updated * WIRE_SCALE).astype(WIRE)
    got = lax.ppermute(sent, "block", [(i, (i + 1) % count) for i in range(count)])
    return got.astype(F32) * (1.0 / WIRE_SCALE)


def local(fast_in, queries, keys, values, rates):
    steps = queries.shape[0]
    tok = lax.axis_index("tok").astype(jnp.int32)[None]
    batches = []
    first = exchange(pack(tok, [(keys, 0), (values, 0)], rates))
    batches.append(first)
    previous = first
    for s in range(1, steps):
        packed = pack(tok, [(keys, s), (values, s), (queries, s - 1)])
        packed, _ = lax.optimization_barrier((packed, previous))
        previous = exchange(packed)
        batches.append(previous)
    packed = pack(tok, [(queries, steps - 1)])
    packed, _ = lax.optimization_barrier((packed, previous))
    last = exchange(packed)
    weights = fast_in[0, 0]
    outputs = None
    for s in range(steps):
        updated = update(weights, batches[s], first, s, 0)
        if s < steps - 1:
            weights = handed_on(updated)
            pieces = apply_fast(updated, batches[s + 1], 256)
        else:
            pieces = apply_fast(updated, last, 0)
        outputs = place(tok, exchange(pieces), s, steps, outputs)
    return (outputs, updated[None, None])


def solution(mesh):
    tokens = P(None, "block", "tok", None)
    weights = P("block", "tok", None, None, None)
    return jax.shard_map(
        local,
        mesh=mesh,
        in_specs=(weights, tokens, tokens, tokens, tokens),
        out_specs=(tokens, weights),
        check_vma=False,
    )
```
